32 devices in a mesh: copy: 2 (over y), grid: 4 (over z), blk: 2 (over x), sub: 2 (over core).
Axes of the slice: x: 2, y: 2, z: 4, core: 2. Of those that a mesh axis runs over, the one named last changes fastest.
Arguments:
- ensemble: float32 [128, 3, 256, 1024], P(('copy', 'grid'), None, 'blk', 'sub'), parts along dimension 0, may hold values from -6 to 6
- basin_thickness: float32 [512, 1024], P(('copy', 'blk'), 'sub'), parts along dimension 0, may hold values from 0.25 to 2
- wet_indicator: int32 [512, 1024], P(('copy', 'blk'), 'sub'), parts along dimension 0, may hold values 0 or 1
- obs_cell: int32 [4, 4, 2, 64], P(('copy', 'blk'), 'grid', 'sub'), parts along dimension 0, may hold values from 0 to 16383
- obs_count: int32 [4, 4, 2], P(('copy', 'blk'), 'grid', 'sub'), parts along dimension 0, may hold values from 16 to 64, as said below
- obs_value: float32 [4, 4, 2, 64], P(('copy', 'blk'), 'grid', 'sub'), parts along dimension 0, may hold values from -6 to 6
- obs_error: float32 [4, 4, 2, 64], P(('copy', 'blk'), 'grid', 'sub'), parts along dimension 0, may hold values from 0.5 to 2
Outputs:
- analysis: float32 [128, 3, 2, 128, 1024], P('copy', None, 'blk', 'grid', 'sub'), parts along dimension 0
The draws below stay inside these ranges and needn't reach their ends.
There are 2 independent parts, one for each index of `copy`. The reference program is written for one: setup_inputs(seed, part) draws one part's arguments, and reference() takes and returns one part's arrays. A program takes and returns all parts, laid end to end along the dimension named above; each array names one. Nothing has to cross between parts.
Inputs may be any that keep to these rules, and one draw needn't show every extreme that they name: `obs_count`: one block of every draw has all 64 slots live.
All inputs are finite; a program needn't handle non-finite values. No bound on the sum of `wet_indicator` on one device may be relied on, other than what follows from the above.
Results may differ from the reference program's by a relative error of at most 0.0003.
Values sent between devices are 32-bit elements; how exact they have to be, the bound alone decides.
No kernel may reach another device: no remote copies, remote signals or barrier semaphores. Data moves between devices by JAX's collectives and lax.ppermute only.
A program may use at most 128 MiB of HBM per device.

```python
import math
import jax
import jax.numpy as jnp
from jax import lax

K = 64
CX = 128
CY = 512
OBS = 64
STEPS = 2
NS_STEPS = 8
RB = 32
NX = 256
NY = 1024
N_GRID = 4
N_BLK = 2
N_SUB = 2


def draw_obs_count(key, part):
    shape = (N_BLK, N_GRID, N_SUB)
    lowest = max(1, OBS // 4)
    counts = jax.random.randint(key, shape, lowest, OBS + 1, dtype=jnp.int32).reshape(-1)
    chosen = jax.random.randint(jax.random.fold_in(key, 7), (), 0, counts.shape[0], dtype=jnp.int32)
    counts = jnp.where(jnp.arange(counts.shape[0], dtype=jnp.int32) == chosen, OBS, counts)
    return counts.reshape(shape).astype(jnp.int32)


def plant(values, key, least, top_value):
    longest = values.shape.index(max(values.shape))
    spots = []
    for shift in (0, 1):
        where = [jax.random.randint(jax.random.fold_in(key, axis), (), 0, length) for axis, length in enumerate(values.shape)]
        where[longest] = (where[longest] + shift) % values.shape[longest]
        spots.append(tuple(where))
    return values.at[spots[0]].set(least).at[spots[1]].set(top_value)


def levels(own_key, dims, pieces, least, largest):
    level = 1.0
    for position, shards_of in pieces:
        steps = jax.random.uniform(jax.random.fold_in(jax.random.fold_in(own_key, 6), position), (shards_of,), jnp.float32, least / len(pieces), largest / len(pieces))
        level = level * jnp.repeat(jnp.exp(steps), dims[position] // shards_of).reshape((-1,) + (1,) * (len(dims) - 1 - position))
    return level


def noise(rng, dims, scale, limit, shards=(), kind=jnp.bfloat16):
    values = jax.random.normal(rng, dims, jnp.float32) * scale
    if len(shards) > 0:
        values = levels(rng, dims, shards, -0.22, 0.18) * values
    return jnp.clip(values, min=-limit, max=limit).astype(kind)


def setup_inputs(seed: int = 0, part: int = 0) -> dict:
    key_of = jax.random.split(jax.random.key(seed), 8)
    own_keys = jax.random.split(jax.random.fold_in(key_of[7], part), 8)
    return {
        "ensemble": noise(own_keys[0], (K, 3, NX, NY), 1.0, 6.0, ((0, 4), (2, 2), (3, 2)), jnp.float32),
        "basin_thickness": jnp.clip(jnp.exp(math.log(2.0) - 2.0794415 * jax.random.uniform(own_keys[1], (NX, NY), jnp.float32) ** levels(own_keys[1], (NX, NY), ((0, 2), (1, 2)), -0.2, 0.2)), 0.25, 2.0),
        "wet_indicator": plant((jax.random.randint(own_keys[2], (NX, NY), 0, 5) < 4).astype(jnp.int32), jax.random.fold_in(own_keys[2], 1), 0, 1),
        "obs_cell": plant(jax.random.randint(own_keys[3], (N_BLK, N_GRID, N_SUB, OBS), 0, RB * CY), jax.random.fold_in(own_keys[3], 1), 0, (RB * CY) - 1).astype(jnp.int32),
        "obs_count": draw_obs_count(jax.random.fold_in(jax.random.fold_in(key_of[7], part), 71), part),
        "obs_value": noise(own_keys[5], (N_BLK, N_GRID, N_SUB, OBS), 1.5, 6.0, ((0, 2), (1, 4), (2, 2)), jnp.float32),
        "obs_error": jnp.clip(jnp.exp(math.log(2.0) - 1.3862944 * jax.random.uniform(own_keys[6], (N_BLK, N_GRID, N_SUB, OBS), jnp.float32) ** levels(own_keys[6], (N_BLK, N_GRID, N_SUB, OBS), ((0, 2), (1, 4), (2, 2)), -0.2, 0.2)), 0.5, 2.0),
    }


FRICTION = 0.05
PRESSURE = 0.35
DIVERGE = 0.35
CORIOLIS = 0.2
precise = lax.Precision.HIGHEST

def along_first(field):
    bordered_array = jnp.pad(field, [(0, 0)] * (field.ndim - 2) + [(1, 1), (0, 0)])
    return bordered_array[..., 2:, :] - bordered_array[..., :-2, :]

def along_second(field):
    bordered_array = jnp.pad(field, [(0, 0)] * (field.ndim - 1) + [(1, 1)])
    return bordered_array[..., 2:] - bordered_array[..., :-2]

def propagate_prior(dynamic_vector, basin_thickness, shore_indicator, latitude_coupling):
    height = dynamic_vector[:, 0]
    first = dynamic_vector[:, 1]
    second = dynamic_vector[:, 2]
    first_new = shore_indicator * ((1.0 - FRICTION) * first + latitude_coupling * second - PRESSURE * along_first(height))
    second_new = shore_indicator * ((1.0 - FRICTION) * second - latitude_coupling * first - PRESSURE * along_second(height))
    height_new = height - DIVERGE * (along_first(basin_thickness * first_new) + along_second(basin_thickness * second_new))
    return jnp.stack([height_new, first_new, second_new], axis=1)

def transform(gram, proj):
    eye = jnp.eye(K, dtype=jnp.float32)
    system = eye + gram
    mean_w = jnp.linalg.solve(system, proj)
    scale = jnp.sqrt(jnp.sum(system * system))
    ystate = system / scale
    zstate = eye
    for sweep in range(NS_STEPS):
        factor = 1.5 * eye - 0.5 * jnp.dot(zstate, ystate, precision=precise)
        ystate = jnp.dot(ystate, factor, precision=precise)
        zstate = jnp.dot(factor, zstate, precision=precise)
    return mean_w[:, None] + zstate / jnp.sqrt(scale)

def reference(ensemble, basin_thickness, wet_indicator, obs_cell, obs_count, obs_value, obs_error):
    shore_indicator = wet_indicator.astype(jnp.float32)
    rows = jnp.arange(NX, dtype=jnp.float32)
    latitude_coupling = (CORIOLIS * (2.0 * (rows + 0.5) / NX - 1.0))[:, None]
    dynamic_vector = ensemble
    for number in range(STEPS):
        dynamic_vector = propagate_prior(dynamic_vector, basin_thickness, shore_indicator, latitude_coupling)
    split = dynamic_vector.reshape(K, 3, N_BLK, N_GRID, RB, NY)

    def domain(index):
        index = index.astype(jnp.int32)
        local = lax.dynamic_index_in_dim(split, index, 3, keepdims=False)
        cells = lax.dynamic_index_in_dim(obs_cell, index, 1, keepdims=False)
        counts = lax.dynamic_index_in_dim(obs_count, index, 1, keepdims=False)
        values = lax.dynamic_index_in_dim(obs_value, index, 1, keepdims=False)
        errors = lax.dynamic_index_in_dim(obs_error, index, 1, keepdims=False)
        surface_height = local[:, 0].reshape(K, N_BLK, RB, N_SUB, CY).transpose(0, 1, 3, 2, 4).reshape(K, N_BLK, N_SUB, RB * CY)
        picked = jnp.take_along_axis(surface_height, jnp.broadcast_to(cells[None], (K,) + cells.shape), axis=3).reshape(K, -1)
        pbar = lax.optimization_barrier(jnp.mean(picked, axis=0))
        valid = (jnp.arange(OBS, dtype=jnp.int32)[None, None, :] < counts[:, :, None]).reshape(-1)
        scale = jnp.where(valid, 1.0 / (errors.reshape(-1) * math.sqrt(K - 1)), 0.0)
        anomobs = (picked - pbar) * scale
        innov = (values.reshape(-1) - pbar) * scale
        gram = jnp.dot(anomobs, anomobs.T, precision=precise)
        proj = jnp.dot(anomobs, innov, precision=precise)
        weights = transform(gram, proj)
        flat = local.reshape(K, -1)
        center = lax.optimization_barrier(jnp.mean(flat, axis=0))
        member_deviations = flat - center
        return (center + jnp.dot(weights.T, member_deviations, precision=precise)).reshape(K, 3, N_BLK, RB, NY)
    results = lax.map(domain, jnp.arange(N_GRID, dtype=jnp.int32))
    return results.transpose(1, 2, 3, 0, 4, 5).reshape(K, 3, N_BLK, CX, NY)
```

```python
import functools
import math

import jax
import jax.numpy as jnp
from jax import lax
from jax.experimental import pallas as pl
from jax.experimental.pallas import tpu as pltpu
from jax.sharding import PartitionSpec as P

STEPS = 2
NS_STEPS = 8
FRICTION = 0.05
PRESSURE = 0.35
DIVERGE = 0.35
CORIOLIS = 0.2
HALO = 2 * STEPS
PAD = 8
LANES = 128
f32 = jnp.float32


def thirds(x):
    top = x.astype(jnp.bfloat16)
    x = x - top.astype(f32)
    middle = x.astype(jnp.bfloat16)
    return top, middle, (x - middle.astype(f32)).astype(jnp.bfloat16)


def product(a, b, dims):
    dot = lambda x, y: lax.dot_general(x, y, (dims, ((), ())), preferred_element_type=f32)
    if a.dtype == jnp.bfloat16:
        return dot(a, b)
    (a0, a1, a2), (b0, b1, b2) = thirds(a), thirds(b)
    return ((dot(a2, b0) + dot(a0, b2)) + dot(a1, b1)) + (dot(a1, b0) + dot(a0, b1)) + dot(a0, b0)


def nt(a, b):
    return product(a, b, ((1,), (1,)))


def nn(a, b):
    return product(a, b, ((1,), (0,)))


def pack_kernel(*refs, members, two, statics):
    ens_head, ens_tail, ens_first, ens_last, ens_hf, ens_hl, ens_tf, ens_tl = refs[:8]
    refs = refs[8:]
    if statics:
        thick, wet = refs[:2]
        refs = refs[2:]
    outs = refs
    b, s = lax.axis_index("blk"), lax.axis_index("sub")
    step = pl.program_id(0)

    def emit(head, tail, first, last, corner_head, corner_tail, index):
        if two:
            outs[0][0, index] = jnp.where(b == 0, tail, head)
            outs[1][0, index] = jnp.where(b == 0, corner_tail, corner_head)
        else:
            outs[0][0, index] = head
            outs[1][0, index] = corner_head
            outs[2][0, index] = tail
            outs[3][0, index] = corner_tail
        outs[-1][0, index] = jnp.where(s == 0, last, first)

    def member():
        for field in range(3):
            emit(
                ens_head[0, field, :HALO],
                ens_tail[0, field, PAD - HALO :],
                ens_first[0, field],
                ens_last[0, field],
                jnp.where(s == 0, ens_hl[0, field, :HALO], ens_hf[0, field, :HALO]),
                jnp.where(s == 0, ens_tl[0, field, PAD - HALO :], ens_tf[0, field, PAD - HALO :]),
                field,
            )

    if not statics:
        member()
        return

    pl.when(step < members)(member)

    @pl.when(step == members)
    def _():
        for index, source in enumerate((thick[...], wet[...].astype(f32))):
            rows, columns = source.shape
            head, tail = source[:HALO], source[rows - HALO :]
            first, last = source[:, :LANES], source[:, columns - LANES :]
            emit(
                head,
                tail,
                first,
                last,
                jnp.where(s == 0, head[:, columns - LANES :], head[:, :LANES]),
                jnp.where(s == 0, tail[:, columns - LANES :], tail[:, :LANES]),
                index,
            )


def edges(ensemble, first, members, statics):
    rows, columns = ensemble.shape[2:]
    two = lax.axis_size("blk") == 2
    held = members + (1 if statics else 0)
    row_end, column_end = rows // PAD - 1, columns // LANES - 1

    def taken(block, r, c):
        return pl.BlockSpec((1, 3) + block, lambda i: (first + jnp.minimum(i, members - 1), 0, r, c))

    in_specs = [
        taken((PAD, columns), 0, 0),
        taken((PAD, columns), row_end, 0),
        taken((rows, LANES), 0, 0),
        taken((rows, LANES), 0, column_end),
        taken((PAD, LANES), 0, 0),
        taken((PAD, LANES), 0, column_end),
        taken((PAD, LANES), row_end, 0),
        taken((PAD, LANES), row_end, column_end),
    ]
    operands = [ensemble] * 8
    if statics:
        in_specs += [pl.BlockSpec((rows, columns), lambda i: (0, 0))] * 2
        operands += list(statics)
    shapes = [(3, HALO, columns), (3, HALO, LANES)] * (1 if two else 2) + [(3, rows, LANES)]
    packed = pl.pallas_call(
        functools.partial(pack_kernel, members=members, two=two, statics=bool(statics)),
        grid=(held,),
        in_specs=in_specs,
        out_specs=[pl.BlockSpec((1,) + s, lambda i: (i, 0, 0, 0)) for s in shapes],
        out_shape=[jax.ShapeDtypeStruct((held,) + s, f32) for s in shapes],
        name="edges",
    )(*operands)
    return halo(packed)


def halo(packed):
    count = lax.axis_size("blk")
    beside = lax.ppermute(packed[-1], "sub", [(0, 1), (1, 0)])
    if count == 2:
        lines = lax.ppermute(packed[0], "blk", [(0, 1), (1, 0)])
        corners = lax.ppermute(packed[1], ("blk", "sub"), [(0, 3), (3, 0), (1, 2), (2, 1)])
        return lines, lines, beside, corners, corners
    up = [(i + 1, i) for i in range(count - 1)]
    down = [(i, i + 1) for i in range(count - 1)]
    below = lax.ppermute(packed[0], "blk", up)
    above = lax.ppermute(packed[2], "blk", down)
    cross = lambda pairs: [(2 * i + s, 2 * j + 1 - s) for i, j in pairs for s in (0, 1)]
    corners_below = lax.ppermute(packed[1], ("blk", "sub"), cross(up))
    corners_above = lax.ppermute(packed[3], ("blk", "sub"), cross(down))
    return below, above, beside, corners_below, corners_above


def forecast_kernel(*refs, parts, tiles, lines, ranges):
    ens, thick, wet = refs[:3]
    mem_halo, sta_halo = refs[3:8], refs[8:13]
    n_out = parts * len(ranges)
    outs = refs[13 : 13 + n_out]
    h, u, v, fu, g, m95, mf, m35, t35, inside, res = refs[13 + n_out :]
    rows, columns = thick.shape
    height, width = h.shape
    z, b, s = lax.axis_index("grid"), lax.axis_index("blk"), lax.axis_index("sub")
    lane = lax.broadcasted_iota(jnp.int32, (1, LANES), 1)
    beside_ok = jnp.where(lax.div(lane, LANES // 2) == s, 1.0, 0.0)
    below_ok = (b < tiles - 1).astype(f32)
    above_ok = (b > 0).astype(f32)
    lower = rows + PAD

    def place(ref, center, below, above, beside, corner_below, corner_above):
        ref[PAD:lower, :columns] = center
        ref[PAD:lower, columns:] = beside * beside_ok
        ref[lower : lower + HALO, :columns] = below * below_ok
        ref[PAD - HALO : PAD, :columns] = above * above_ok
        ref[lower : lower + HALO, columns:] = corner_below * beside_ok * below_ok
        ref[PAD - HALO : PAD, columns:] = corner_above * beside_ok * above_ok

    @pl.when(pl.program_id(0) == 0)
    def _():
        for ref in (h, u, v, m95, t35, inside):
            ref[:PAD] = jnp.zeros((PAD, width), f32)
            ref[lower:] = jnp.zeros((PAD, width), f32)
        place(t35, thick[...], *(ref[0, 0] for ref in sta_halo))
        place(m95, wet[...].astype(f32), *(ref[0, 1] for ref in sta_halo))
        one = lambda *shape: jnp.ones(shape, f32)
        place(inside, one(rows, columns), one(HALO, columns), one(HALO, columns), one(rows, LANES), one(HALO, LANES), one(HALO, LANES))
        for r in range(0, height, PAD):
            here = slice(r, r + PAD)
            t35[here] = DIVERGE * t35[here]
            m = m95[here]
            line = (b * rows + (r - PAD) + lax.broadcasted_iota(jnp.int32, (PAD, 1), 0)).astype(f32)
            m95[here] = (1.0 - FRICTION) * m
            m35[here] = PRESSURE * m
            mf[here] = (CORIOLIS * (2.0 * (line + 0.5) / (tiles * rows) - 1.0)) * m

    for field, ref in enumerate((h, u, v)):
        place(ref, ens[0, field], *(halo_ref[0, field] for halo_ref in mem_halo))

    def above_of(ref, r):
        return pltpu.roll(ref[:PAD], 1, 0) if r == 0 else ref[r - 1 : r - 1 + PAD]

    def below_of(ref, r):
        return pltpu.roll(ref[r : r + PAD], PAD - 1, 0) if r + PAD == height else ref[r + 1 : r + 1 + PAD]

    def across(field):
        return pltpu.roll(field, width - 1, 1) - pltpu.roll(field, 1, 1)

    def keep(field, r, value):
        size = min(PAD, lines)
        for start in range(0, PAD, size):
            domain, line = divmod(r - PAD + start, lines)
            res[field, domain, line : line + size] = value[start : start + size, :columns]

    for step in range(STEPS):
        last = step == STEPS - 1
        for r in range(0, height, PAD):
            here = slice(r, r + PAD)
            hc, uc, vc = h[here], u[here], v[here]
            a, c, d = m95[here], mf[here], m35[here]
            un = a * uc + c * vc - d * (below_of(h, r) - above_of(h, r))
            vn = a * vc - c * uc - d * across(hc)
            t = t35[here]
            fu[here] = t * un
            inner = PAD <= r < lower
            if last and inner:
                keep(1, r, un)
                keep(2, r, vn)
            if not last:
                u[here] = un
                v[here] = vn
            if inner or not last:
                g[here] = across(t * vn)
        for r in range(0, height, PAD):
            here = slice(r, r + PAD)
            if last and not PAD <= r < lower:
                continue
            hn = h[here] - ((below_of(fu, r) - above_of(fu, r)) + g[here])
            if last:
                keep(0, r, hn)
            else:
                h[here] = hn * inside[here]

    per_field = outs[0].shape[1] and lines // outs[0].shape[2]
    for shift in range(parts):
        domain = lax.rem(z + shift, parts)
        for number, (start, stop) in enumerate(ranges):
            out = outs[number * parts + shift]
            for q in range(start, stop):
                field, piece = divmod(q, per_field)
                size = out.shape[2]
                out[0, q - start] = res[field, domain, piece * size : (piece + 1) * size]


def forecast(ensemble, first, members, fields, mem_halo, sta_halo, static_at, size, ranges):
    thick, wet = fields
    rows, columns = ensemble.shape[2:]
    parts, tiles = lax.axis_size("grid"), lax.axis_size("blk")
    lines = rows // parts
    ext = pltpu.VMEM((rows + 2 * PAD, columns + LANES), f32)
    whole = pl.BlockSpec((rows, columns), lambda i: (0, 0))
    in_specs = [pl.BlockSpec((1, 3, rows, columns), lambda i: (first + i, 0, 0, 0)), whole, whole]
    in_specs += [pl.BlockSpec((1,) + x.shape[1:], lambda i: (i, 0, 0, 0)) for x in mem_halo]
    in_specs += [pl.BlockSpec((1,) + x.shape[1:], lambda i: (static_at, 0, 0, 0)) for x in sta_halo]
    shapes = [(stop - start, size, columns) for start, stop in ranges for shift in range(parts)]
    flat = pl.pallas_call(
        functools.partial(forecast_kernel, parts=parts, tiles=tiles, lines=lines, ranges=ranges),
        grid=(members,),
        in_specs=in_specs,
        out_specs=[pl.BlockSpec((1,) + s, lambda i: (i, 0, 0, 0)) for s in shapes],
        out_shape=[jax.ShapeDtypeStruct((members,) + s, f32) for s in shapes],
        scratch_shapes=[ext] * 10 + [pltpu.VMEM((3, parts, lines, columns), f32)],
        compiler_params=pltpu.CompilerParams(vmem_limit_bytes=48 << 20),
        name="forecast",
    )(ensemble, thick, wet, *mem_halo, *sta_halo)
    return [flat[i * parts : (i + 1) * parts] for i in range(len(ranges))]


def exchange(pieces):
    parts = len(pieces)
    got = [pieces[0]]
    for shift in range(1, parts):
        got.append(lax.ppermute(pieces[shift], "grid", [(i, (i + shift) % parts) for i in range(parts)]))
    return got


def rows_of(refs):
    return jnp.concatenate([ref[:, 0].reshape(-1, ref.shape[3]) for ref in refs], axis=0)


def observe_kernel(*refs, members, width):
    count, cell, value, error = refs[:4]
    pieces, (out, picked) = refs[4:-2], refs[-2:]
    q = pl.program_id(0)
    columns = width
    slots = cell.shape[1]
    cells = cell[...]
    column = lax.rem(cells, columns)
    line = lax.rem(lax.div(cells, columns), PAD)
    block = lax.div(cells, columns * PAD)
    chosen = (lax.broadcasted_iota(jnp.int32, (columns, slots), 0) == column) & (block == q)
    pick = jnp.where(chosen, 1.0, 0.0).astype(jnp.bfloat16)
    left = rows_of(pieces)
    found = 0.0
    for part in range(3):
        head = left.astype(jnp.bfloat16)
        found = found + nn(head, pick)
        left = left - head.astype(f32)
    line_of = lax.rem(lax.broadcasted_iota(jnp.int32, found.shape, 0), PAD)
    found = jnp.sum(jnp.where(line_of == line, found, 0.0).reshape(members, PAD, slots), axis=1)

    @pl.when(q == 0)
    def _():
        picked[...] = found

    @pl.when(q > 0)
    def _():
        picked[...] += found

    @pl.when(q == pl.num_programs(0) - 1)
    def _():
        p = picked[...]
        pbar = jnp.mean(p, axis=0, keepdims=True)
        valid = lax.broadcasted_iota(jnp.int32, (1, slots), 1) < count[0, 0]
        scale = jnp.where(valid, 1.0 / (error[...] * math.sqrt(members - 1)), 0.0)
        anomaly = (p - pbar) * scale
        innovation = (value[...] - pbar) * scale
        out[:members] = nt(anomaly, anomaly)
        out[members:] = nt(jnp.broadcast_to(innovation, (PAD, slots)), anomaly)


def piece_specs(pieces, offset):
    return [pl.BlockSpec((x.shape[0], 1) + x.shape[2:], lambda q, o=o: (0, q + o, 0, 0)) for x, o in zip(pieces, offset)]


def observe(pieces, count_q, members, cell, count, value, error):
    slots = cell.shape[-1]
    row = pl.BlockSpec((1, slots), lambda q: (0, 0))
    return pl.pallas_call(
        functools.partial(observe_kernel, members=members, width=pieces[0].shape[3]),
        grid=(count_q,),
        in_specs=[pl.BlockSpec(memory_space=pltpu.SMEM), row, row, row] + piece_specs(pieces, [0] * len(pieces)),
        out_specs=pl.BlockSpec((members + PAD, members), lambda q: (0, 0)),
        out_shape=jax.ShapeDtypeStruct((members + PAD, members), f32),
        scratch_shapes=[pltpu.VMEM((members, slots), f32)],
        name="observe",
    )(count.reshape(1, 1), cell.reshape(1, slots), value.reshape(1, slots), error.reshape(1, slots), *pieces)


def transform_kernel(packed, high, low, *, parts, members):
    each = members // parts
    z = lax.axis_index("grid")
    row = lax.broadcasted_iota(jnp.int32, (members, members), 0)
    col = lax.broadcasted_iota(jnp.int32, (members, members), 1)
    eye = jnp.where(row == col, 1.0, 0.0)
    system = eye + packed[:members]
    proj = nt(eye, packed[members:])[:, :1]
    wide = 2 * members
    lane = lax.broadcasted_iota(jnp.int32, (members, wide), 1)
    sub = lax.broadcasted_iota(jnp.int32, (members, wide), 0)
    tableau = jnp.concatenate([system, jnp.broadcast_to(proj, (members, members))], axis=1)

    def eliminate(p, a):
        pivot_row = jnp.sum(jnp.where(sub == p, a, 0.0), axis=0, keepdims=True)
        column = jnp.sum(jnp.where(lane == p, a, 0.0), axis=1, keepdims=True)
        pivot = jnp.sum(jnp.where(lane[:1] == p, pivot_row, 0.0), axis=1, keepdims=True)
        pivot_row = pivot_row / pivot
        return jnp.where(sub == p, pivot_row, a - column * pivot_row)

    tableau = lax.fori_loop(0, members, eliminate, tableau)
    mean_w = jnp.sum(jnp.where(lane == members, tableau, 0.0), axis=1, keepdims=True)
    total = jnp.sum(jnp.sum(system * system, axis=1, keepdims=True), axis=0, keepdims=True)
    scale = jnp.sqrt(total)

    def sweep(_, state):
        y, zz = state
        factor = 1.5 * eye - 0.5 * nn(zz, y)
        return nn(y, factor), nn(factor, zz)

    _, zz = lax.fori_loop(0, NS_STEPS, sweep, (system / scale, eye))
    weights = mean_w + zz / jnp.sqrt(scale)
    mix = weights - jnp.mean(weights, axis=0, keepdims=True) + 1.0 / members
    place, item = lax.div(col, each), lax.rem(col, each)
    true = lax.rem(z - place + parts, parts) * each + item
    mixed = nt(jnp.where(row == true, 1.0, 0.0), mix)
    tall = members * PAD
    spread = jnp.where(
        lax.div(lax.broadcasted_iota(jnp.int32, (tall, members), 0), PAD)
        == lax.broadcasted_iota(jnp.int32, (tall, members), 1),
        1.0,
        0.0,
    ).astype(jnp.bfloat16)
    same = lax.rem(lax.broadcasted_iota(jnp.int32, (tall, tall), 0), PAD) == lax.rem(
        lax.broadcasted_iota(jnp.int32, (tall, tall), 1), PAD
    )
    top = mixed.astype(jnp.bfloat16)
    rest = (mixed - top.astype(f32)).astype(jnp.bfloat16)
    for out, part in ((high, top), (low, rest)):
        tallened = nn(spread, part).astype(jnp.bfloat16)
        out[...] = jnp.where(same, nt(tallened, spread), 0.0).astype(jnp.bfloat16)


def transform(packed, members):
    parts = lax.axis_size("grid")
    tall = members * PAD
    shape = jax.ShapeDtypeStruct((tall, tall), jnp.bfloat16)
    return pl.pallas_call(
        functools.partial(transform_kernel, parts=parts, members=members),
        out_shape=[shape, shape],
        name="transform",
    )(packed)


def analysis_kernel(*refs, carried):
    high, low = refs[:2]
    pieces, out = refs[2 : -1 - carried], refs[-1]
    x = rows_of(pieces)
    top = x.astype(jnp.bfloat16)
    rest = (x - top.astype(f32)).astype(jnp.bfloat16)
    y = nn(high[...], rest) + nn(low[...], top)
    y = y + nn(high[...], top)
    out[...] = y.reshape(out.shape)


def analyse(mixers, pieces, offset, q0, q1, shape, carried):
    square = pl.BlockSpec(mixers[0].shape, lambda q: (0, 0))
    specs = [square, square] + piece_specs(pieces, offset)
    operands = [*mixers, *pieces]
    aliases = {}
    if carried is not None:
        aliases = {len(operands): 0}
        specs.append(pl.BlockSpec(memory_space=pl.ANY))
        operands.append(carried)
    return pl.pallas_call(
        functools.partial(analysis_kernel, carried=int(carried is not None)),
        grid=(q1 - q0,),
        in_specs=specs,
        out_specs=pl.BlockSpec((shape[0], 1) + shape[2:], lambda q: (0, q + q0, 0, 0)),
        out_shape=jax.ShapeDtypeStruct(shape, f32),
        input_output_aliases=aliases,
        name="analysis",
    )(*operands)


def shards(ensemble, basin_thickness, wet_indicator, obs_cell, obs_count, obs_value, obs_error):
    held, _, rows, columns = ensemble.shape
    parts = lax.axis_size("grid")
    members = held * parts
    lines = rows // parts
    size = PAD if lines % PAD == 0 else lines
    per_field = lines // size
    total = 3 * per_field
    width = size * columns // PAD
    early = max(1, held // 4)
    late = held - early
    fields = (basin_thickness, wet_indicator)
    halo_early = edges(ensemble, 0, early, fields)
    halo_late = edges(ensemble, early, late, ())
    ranges_early = [(0, per_field), (per_field, total)]
    cuts = sorted({0, per_field, 2 * per_field, total - 1, total})
    ranges_late = list(zip(cuts[:-1], cuts[1:]))
    sent_early = forecast(ensemble, 0, early, fields, halo_early, halo_early, early, size, ranges_early)
    sent_late = forecast(ensemble, early, late, fields, halo_late, halo_early, early, size, ranges_late)

    def received(pieces):
        got = exchange(pieces)
        return [x.reshape(x.shape[0], x.shape[1], PAD, width) for x in got]

    early_h = received(sent_early[0])
    late_h = received(sent_late[0])
    early_uv = received(sent_early[1])
    late_uv = [received(x) for x in sent_late[1:]]

    def woven(a, b):
        return [x for pair in zip(a, b) for x in pair]

    packed = observe(woven(early_h, late_h), per_field, members, obs_cell, obs_count, obs_value, obs_error)
    packed = lax.psum(packed, ("blk", "sub"))
    mixers = transform(packed, members)
    shape = (members, total, PAD, width)
    out = analyse(mixers, woven(early_h, late_h), [0] * (2 * parts), 0, per_field, shape, None)
    for (start, stop), pieces in zip(ranges_late[1:], late_uv):
        offset = [start - per_field, 0] * parts
        out = analyse(mixers, woven(early_uv, pieces), offset, start, stop, shape, out)
    return out.reshape(members, 3, 1, lines, columns)


def solution(mesh):
    placed = (
        P(("copy", "grid"), None, "blk", "sub"),
        P(("copy", "blk"), "sub"),
        P(("copy", "blk"), "sub"),
        P(("copy", "blk"), "grid", "sub"),
        P(("copy", "blk"), "grid", "sub"),
        P(("copy", "blk"), "grid", "sub"),
        P(("copy", "blk"), "grid", "sub"),
    )
    return jax.shard_map(
        shards,
        mesh=mesh,
        in_specs=placed,
        out_specs=P("copy", None, "blk", "grid", "sub"),
        check_vma=False,
    )
```

```python
import functools
import math

import jax
import jax.numpy as jnp
from jax import lax
from jax.experimental import pallas as pl
from jax.experimental.pallas import tpu as pltpu
from jax.sharding import PartitionSpec as P

STEPS = 2
NS_STEPS = 8
FRICTION = 0.05
PRESSURE = 0.35
DIVERGE = 0.35
CORIOLIS = 0.2
HALO = 2 * STEPS
PAD = 8
LANES = 128
f32 = jnp.float32


def cost(us):
    return pl.CostEstimate(flops=int(us * 1e6), transcendentals=0, bytes_accessed=int(us * 3e3))


def tied(values, *earlier):
    return lax.optimization_barrier((values, earlier))[0]


def thirds(x):
    top = x.astype(jnp.bfloat16)
    x = x - top.astype(f32)
    middle = x.astype(jnp.bfloat16)
    return top, middle, (x - middle.astype(f32)).astype(jnp.bfloat16)


def product(a, b, dims):
    dot = lambda x, y: lax.dot_general(x, y, (dims, ((), ())), preferred_element_type=f32)
    if a.dtype == jnp.bfloat16:
        return dot(a, b)
    (a0, a1, a2), (b0, b1, b2) = thirds(a), thirds(b)
    return ((dot(a2, b0) + dot(a0, b2)) + dot(a1, b1)) + (dot(a1, b0) + dot(a0, b1)) + dot(a0, b0)


def nt(a, b):
    return product(a, b, ((1,), (1,)))


def nn(a, b):
    return product(a, b, ((1,), (0,)))


def pack_kernel(*refs, chunk, two, statics, waits):
    ens_head, ens_tail, ens_first, ens_last, ens_hf, ens_hl, ens_tf, ens_tl = refs[:8]
    outs = refs[8 + (2 if statics else 0) + waits :]
    b, s = lax.axis_index("blk"), lax.axis_index("sub")

    def emit(head, tail, first, last, corner_head, corner_tail, i, index):
        if two:
            outs[0][i, index] = jnp.where(b == 0, tail, head)
            outs[1][i, index] = jnp.where(b == 0, corner_tail, corner_head)
        else:
            outs[0][i, index] = head
            outs[1][i, index] = corner_head
            outs[2][i, index] = tail
            outs[3][i, index] = corner_tail
        outs[-1][i, index] = jnp.where(s == 0, last, first)

    for i in range(chunk):
        for field in range(3):
            emit(
                ens_head[i, field, :HALO],
                ens_tail[i, field, PAD - HALO :],
                ens_first[i, field],
                ens_last[i, field],
                jnp.where(s == 0, ens_hl[i, field, :HALO], ens_hf[i, field, :HALO]),
                jnp.where(s == 0, ens_tl[i, field, PAD - HALO :], ens_tf[i, field, PAD - HALO :]),
                i,
                field,
            )
    if statics:
        for index, source in enumerate((refs[8][...], refs[9][...].astype(f32))):
            rows, columns = source.shape
            head, tail = source[:HALO], source[rows - HALO :]
            first, last = source[:, :LANES], source[:, columns - LANES :]
            emit(
                head,
                tail,
                first,
                last,
                jnp.where(s == 0, head[:, columns - LANES :], head[:, :LANES]),
                jnp.where(s == 0, tail[:, columns - LANES :], tail[:, :LANES]),
                chunk,
                index,
            )


def edges(ensemble, first, members, statics, after):
    rows, columns = ensemble.shape[2:]
    two = lax.axis_size("blk") == 2
    chunk = math.gcd(first, members) if not statics else members
    held = members + (1 if statics else 0)
    block = chunk + (1 if statics else 0)
    row_end, column_end = rows // PAD - 1, columns // LANES - 1

    def taken(shape, r, c):
        return pl.BlockSpec((chunk, 3) + shape, lambda i: (first // chunk + i, 0, r, c))

    in_specs = [
        taken((PAD, columns), 0, 0),
        taken((PAD, columns), row_end, 0),
        taken((rows, LANES), 0, 0),
        taken((rows, LANES), 0, column_end),
        taken((PAD, LANES), 0, 0),
        taken((PAD, LANES), 0, column_end),
        taken((PAD, LANES), row_end, 0),
        taken((PAD, LANES), row_end, column_end),
    ]
    in_specs += [pl.BlockSpec((rows, columns), lambda i: (0, 0))] * len(statics)
    in_specs += [pl.BlockSpec(memory_space=pl.ANY)] * len(after)
    shapes = [(3, HALO, columns), (3, HALO, LANES)] * (1 if two else 2) + [(3, rows, LANES)]
    packed = pl.pallas_call(
        functools.partial(pack_kernel, chunk=chunk, two=two, statics=bool(statics), waits=len(after)),
        grid=(members // chunk,),
        in_specs=in_specs,
        out_specs=[pl.BlockSpec((block,) + s, lambda i: (i, 0, 0, 0)) for s in shapes],
        out_shape=[jax.ShapeDtypeStruct((held,) + s, f32) for s in shapes],
        cost_estimate=cost(3),
        name="edges",
    )(*[ensemble] * 8, *statics, *after)
    return halo(packed)


def halo(packed):
    count = lax.axis_size("blk")
    beside = lax.ppermute(packed[-1], "sub", [(0, 1), (1, 0)])
    if count == 2:
        lines = lax.ppermute(packed[0], "blk", [(0, 1), (1, 0)])
        corners = lax.ppermute(packed[1], ("blk", "sub"), [(0, 3), (3, 0), (1, 2), (2, 1)])
        return lines, lines, beside, corners, corners
    up = [(i + 1, i) for i in range(count - 1)]
    down = [(i, i + 1) for i in range(count - 1)]
    below = lax.ppermute(packed[0], "blk", up)
    above = lax.ppermute(packed[2], "blk", down)
    cross = lambda pairs: [(2 * i + s, 2 * j + 1 - s) for i, j in pairs for s in (0, 1)]
    corners_below = lax.ppermute(packed[1], ("blk", "sub"), cross(up))
    corners_above = lax.ppermute(packed[3], ("blk", "sub"), cross(down))
    return below, above, beside, corners_below, corners_above


def forecast_kernel(*refs, parts, tiles, lines, ranges):
    ens, thick, wet = refs[:3]
    mem_halo, sta_halo = refs[3:8], refs[8:13]
    n_out = parts * len(ranges)
    outs = refs[13 : 13 + n_out]
    h, u, v, fu, g, m95, mf, m35, t35, inside, res = refs[13 + n_out :]
    rows, columns = thick.shape
    height, width = h.shape
    z, b, s = lax.axis_index("grid"), lax.axis_index("blk"), lax.axis_index("sub")
    lane = lax.broadcasted_iota(jnp.int32, (1, LANES), 1)
    beside_ok = jnp.where(lax.div(lane, LANES // 2) == s, 1.0, 0.0)
    below_ok = (b < tiles - 1).astype(f32)
    above_ok = (b > 0).astype(f32)
    lower = rows + PAD

    def place(ref, center, below, above, beside, corner_below, corner_above):
        ref[PAD:lower, :columns] = center
        ref[PAD:lower, columns:] = beside * beside_ok
        ref[lower : lower + HALO, :columns] = below * below_ok
        ref[PAD - HALO : PAD, :columns] = above * above_ok
        ref[lower : lower + HALO, columns:] = corner_below * beside_ok * below_ok
        ref[PAD - HALO : PAD, columns:] = corner_above * beside_ok * above_ok

    @pl.when(pl.program_id(0) == 0)
    def _():
        for ref in (h, u, v, m95, t35, inside):
            ref[:PAD] = jnp.zeros((PAD, width), f32)
            ref[lower:] = jnp.zeros((PAD, width), f32)
        place(t35, thick[...], *(ref[0, 0] for ref in sta_halo))
        place(m95, wet[...].astype(f32), *(ref[0, 1] for ref in sta_halo))
        one = lambda *shape: jnp.ones(shape, f32)
        place(inside, one(rows, columns), one(HALO, columns), one(HALO, columns), one(rows, LANES), one(HALO, LANES), one(HALO, LANES))
        for r in range(0, height, PAD):
            here = slice(r, r + PAD)
            t35[here] = DIVERGE * t35[here]
            m = m95[here]
            line = (b * rows + (r - PAD) + lax.broadcasted_iota(jnp.int32, (PAD, 1), 0)).astype(f32)
            m95[here] = (1.0 - FRICTION) * m
            m35[here] = PRESSURE * m
            mf[here] = (CORIOLIS * (2.0 * (line + 0.5) / (tiles * rows) - 1.0)) * m

    for field, ref in enumerate((h, u, v)):
        place(ref, ens[0, field], *(halo_ref[0, field] for halo_ref in mem_halo))

    def above_of(ref, r):
        return pltpu.roll(ref[:PAD], 1, 0) if r == 0 else ref[r - 1 : r - 1 + PAD]

    def below_of(ref, r):
        return pltpu.roll(ref[r : r + PAD], PAD - 1, 0) if r + PAD == height else ref[r + 1 : r + 1 + PAD]

    def across(field):
        return pltpu.roll(field, width - 1, 1) - pltpu.roll(field, 1, 1)

    def keep(field, r, value):
        size = min(PAD, lines)
        for start in range(0, PAD, size):
            domain, line = divmod(r - PAD + start, lines)
            res[field, domain, line : line + size] = value[start : start + size, :columns]

    for step in range(STEPS):
        last = step == STEPS - 1
        for r in range(0, height, PAD):
            here = slice(r, r + PAD)
            hc, uc, vc = h[here], u[here], v[here]
            a, c, d = m95[here], mf[here], m35[here]
            un = a * uc + c * vc - d * (below_of(h, r) - above_of(h, r))
            vn = a * vc - c * uc - d * across(hc)
            t = t35[here]
            fu[here] = t * un
            inner = PAD <= r < lower
            if last and inner:
                keep(1, r, un)
                keep(2, r, vn)
            if not last:
                u[here] = un
                v[here] = vn
            if inner or not last:
                g[here] = across(t * vn)
        for r in range(0, height, PAD):
            here = slice(r, r + PAD)
            if last and not PAD <= r < lower:
                continue
            hn = h[here] - ((below_of(fu, r) - above_of(fu, r)) + g[here])
            if last:
                keep(0, r, hn)
            else:
                h[here] = hn * inside[here]

    per_field = outs[0].shape[1] and lines // outs[0].shape[2]
    for shift in range(parts):
        domain = lax.rem(z + shift, parts)
        for number, (start, stop) in enumerate(ranges):
            out = outs[number * parts + shift]
            for q in range(start, stop):
                field, piece = divmod(q, per_field)
                size = out.shape[2]
                out[0, q - start] = res[field, domain, piece * size : (piece + 1) * size]


def forecast(ensemble, first, members, fields, mem_halo, halo_first, sta_halo, static_at, size, ranges):
    thick, wet = fields
    rows, columns = ensemble.shape[2:]
    parts, tiles = lax.axis_size("grid"), lax.axis_size("blk")
    lines = rows // parts
    ext = pltpu.VMEM((rows + 2 * PAD, columns + LANES), f32)
    whole = pl.BlockSpec((rows, columns), lambda i: (0, 0))
    in_specs = [pl.BlockSpec((1, 3, rows, columns), lambda i: (first + i, 0, 0, 0)), whole, whole]
    in_specs += [pl.BlockSpec((1,) + x.shape[1:], lambda i: (halo_first + i, 0, 0, 0)) for x in mem_halo]
    in_specs += [pl.BlockSpec((1,) + x.shape[1:], lambda i: (static_at, 0, 0, 0)) for x in sta_halo]
    shapes = [(stop - start, size, columns) for start, stop in ranges for shift in range(parts)]
    flat = pl.pallas_call(
        functools.partial(forecast_kernel, parts=parts, tiles=tiles, lines=lines, ranges=ranges),
        grid=(members,),
        in_specs=in_specs,
        out_specs=[pl.BlockSpec((1,) + s, lambda i: (i, 0, 0, 0)) for s in shapes],
        out_shape=[jax.ShapeDtypeStruct((members,) + s, f32) for s in shapes],
        scratch_shapes=[ext] * 10 + [pltpu.VMEM((3, parts, lines, columns), f32)],
        compiler_params=pltpu.CompilerParams(vmem_limit_bytes=48 << 20),
        cost_estimate=cost(3 * members),
        name="forecast",
    )(ensemble, thick, wet, *mem_halo, *sta_halo)
    return [flat[i * parts : (i + 1) * parts] for i in range(len(ranges))]


def exchange(pieces):
    parts = len(pieces)
    got = [pieces[0]]
    for shift in range(1, parts):
        got.append(lax.ppermute(pieces[shift], "grid", [(i, (i + shift) % parts) for i in range(parts)]))
    return got


def rows_of(refs):
    return jnp.concatenate([ref[:, 0].reshape(-1, ref.shape[3]) for ref in refs], axis=0)


def observe_kernel(*refs, members, width):
    count, cell, value, error = refs[:4]
    pieces, (out, picked) = refs[4:-2], refs[-2:]
    q = pl.program_id(0)
    columns = width
    slots = cell.shape[1]
    cells = cell[...]
    column = lax.rem(cells, columns)
    line = lax.rem(lax.div(cells, columns), PAD)
    block = lax.div(cells, columns * PAD)
    chosen = (lax.broadcasted_iota(jnp.int32, (columns, slots), 0) == column) & (block == q)
    pick = jnp.where(chosen, 1.0, 0.0).astype(jnp.bfloat16)
    left = rows_of(pieces)
    found = 0.0
    for part in range(3):
        head = left.astype(jnp.bfloat16)
        found = found + nn(head, pick)
        left = left - head.astype(f32)
    line_of = lax.rem(lax.broadcasted_iota(jnp.int32, found.shape, 0), PAD)
    found = jnp.sum(jnp.where(line_of == line, found, 0.0).reshape(members, PAD, slots), axis=1)

    @pl.when(q == 0)
    def _():
        picked[...] = found

    @pl.when(q > 0)
    def _():
        picked[...] += found

    @pl.when(q == pl.num_programs(0) - 1)
    def _():
        p = picked[...]
        pbar = jnp.mean(p, axis=0, keepdims=True)
        valid = lax.broadcasted_iota(jnp.int32, (1, slots), 1) < count[0, 0]
        scale = jnp.where(valid, 1.0 / (error[...] * math.sqrt(members - 1)), 0.0)
        anomaly = (p - pbar) * scale
        innovation = (value[...] - pbar) * scale
        out[:members] = nt(anomaly, anomaly)
        out[members:] = nt(jnp.broadcast_to(innovation, (PAD, slots)), anomaly)


def piece_specs(pieces, offset):
    return [pl.BlockSpec((x.shape[0], 1) + x.shape[2:], lambda q, o=o: (0, q + o, 0, 0)) for x, o in zip(pieces, offset)]


def observe(pieces, count_q, members, cell, count, value, error):
    slots = cell.shape[-1]
    row = pl.BlockSpec((1, slots), lambda q: (0, 0))
    return pl.pallas_call(
        functools.partial(observe_kernel, members=members, width=pieces[0].shape[3]),
        grid=(count_q,),
        in_specs=[pl.BlockSpec(memory_space=pltpu.SMEM), row, row, row] + piece_specs(pieces, [0] * len(pieces)),
        out_specs=pl.BlockSpec((members + PAD, members), lambda q: (0, 0)),
        out_shape=jax.ShapeDtypeStruct((members + PAD, members), f32),
        scratch_shapes=[pltpu.VMEM((members, slots), f32)],
        cost_estimate=cost(6),
        name="observe",
    )(count.reshape(1, 1), cell.reshape(1, slots), value.reshape(1, slots), error.reshape(1, slots), *pieces)


def transform_kernel(packed, high, low, *, parts, members):
    each = members // parts
    z = lax.axis_index("grid")
    row = lax.broadcasted_iota(jnp.int32, (members, members), 0)
    col = lax.broadcasted_iota(jnp.int32, (members, members), 1)
    eye = jnp.where(row == col, 1.0, 0.0)
    system = eye + packed[:members]
    proj = nt(eye, packed[members:])[:, :1]
    wide = 2 * members
    lane = lax.broadcasted_iota(jnp.int32, (members, wide), 1)
    sub = lax.broadcasted_iota(jnp.int32, (members, wide), 0)
    tableau = jnp.concatenate([system, jnp.broadcast_to(proj, (members, members))], axis=1)

    def eliminate(p, a):
        pivot_row = jnp.sum(jnp.where(sub == p, a, 0.0), axis=0, keepdims=True)
        column = jnp.sum(jnp.where(lane == p, a, 0.0), axis=1, keepdims=True)
        pivot = jnp.sum(jnp.where(lane[:1] == p, pivot_row, 0.0), axis=1, keepdims=True)
        pivot_row = pivot_row / pivot
        return jnp.where(sub == p, pivot_row, a - column * pivot_row)

    tableau = lax.fori_loop(0, members, eliminate, tableau)
    mean_w = jnp.sum(jnp.where(lane == members, tableau, 0.0), axis=1, keepdims=True)
    total = jnp.sum(jnp.sum(system * system, axis=1, keepdims=True), axis=0, keepdims=True)
    scale = jnp.sqrt(total)

    def sweep(_, state):
        y, zz = state
        factor = 1.5 * eye - 0.5 * nn(zz, y)
        return nn(y, factor), nn(factor, zz)

    _, zz = lax.fori_loop(0, NS_STEPS, sweep, (system / scale, eye))
    weights = mean_w + zz / jnp.sqrt(scale)
    mix = weights - jnp.mean(weights, axis=0, keepdims=True) + 1.0 / members
    place, item = lax.div(col, each), lax.rem(col, each)
    true = lax.rem(z - place + parts, parts) * each + item
    mixed = nt(jnp.where(row == true, 1.0, 0.0), mix)
    tall = members * PAD
    spread = jnp.where(
        lax.div(lax.broadcasted_iota(jnp.int32, (tall, members), 0), PAD)
        == lax.broadcasted_iota(jnp.int32, (tall, members), 1),
        1.0,
        0.0,
    ).astype(jnp.bfloat16)
    same = lax.rem(lax.broadcasted_iota(jnp.int32, (tall, tall), 0), PAD) == lax.rem(
        lax.broadcasted_iota(jnp.int32, (tall, tall), 1), PAD
    )
    top = mixed.astype(jnp.bfloat16)
    rest = (mixed - top.astype(f32)).astype(jnp.bfloat16)
    for out, part in ((high, top), (low, rest)):
        tallened = nn(spread, part).astype(jnp.bfloat16)
        out[...] = jnp.where(same, nt(tallened, spread), 0.0).astype(jnp.bfloat16)


def transform(packed, members):
    parts = lax.axis_size("grid")
    tall = members * PAD
    shape = jax.ShapeDtypeStruct((tall, tall), jnp.bfloat16)
    return pl.pallas_call(
        functools.partial(transform_kernel, parts=parts, members=members),
        out_shape=[shape, shape],
        cost_estimate=cost(12),
        name="transform",
    )(packed)


def analysis_kernel(*refs, carried):
    high, low = refs[:2]
    pieces, out = refs[2 : -1 - carried], refs[-1]
    x = rows_of(pieces)
    top = x.astype(jnp.bfloat16)
    rest = (x - top.astype(f32)).astype(jnp.bfloat16)
    y = nn(high[...], rest) + nn(low[...], top)
    y = y + nn(high[...], top)
    out[...] = y.reshape(out.shape)


def analyse(mixers, pieces, offset, q0, q1, shape, carried):
    square = pl.BlockSpec(mixers[0].shape, lambda q: (0, 0))
    specs = [square, square] + piece_specs(pieces, offset)
    operands = [*mixers, *pieces]
    aliases = {}
    if carried is not None:
        aliases = {len(operands): 0}
        specs.append(pl.BlockSpec(memory_space=pl.ANY))
        operands.append(carried)
    return pl.pallas_call(
        functools.partial(analysis_kernel, carried=int(carried is not None)),
        grid=(q1 - q0,),
        in_specs=specs,
        out_specs=pl.BlockSpec((shape[0], 1) + shape[2:], lambda q: (0, q + q0, 0, 0)),
        out_shape=jax.ShapeDtypeStruct(shape, f32),
        input_output_aliases=aliases,
        cost_estimate=cost(2 * (q1 - q0)),
        name="analysis",
    )(*operands)


def shards(ensemble, basin_thickness, wet_indicator, obs_cell, obs_count, obs_value, obs_error):
    held, _, rows, columns = ensemble.shape
    parts = lax.axis_size("grid")
    members = held * parts
    lines = rows // parts
    size = PAD if lines % PAD == 0 else lines
    per_field = lines // size
    total = 3 * per_field
    width = size * columns // PAD
    first, early = max(1, held // 16), max(1, held // 4)
    fields = (basin_thickness, wet_indicator)
    cuts = sorted({0, per_field, 2 * per_field, total - 1, total})
    ranges = list(zip(cuts[:-1], cuts[1:]))

    def received(pieces):
        got = exchange(pieces)
        return [x.reshape(x.shape[0], x.shape[1], PAD, width) for x in got]

    halo_early = edges(ensemble, 0, early, fields, ())
    groups, starts = [], []
    for start, stop in [(0, first)] + ([(first, early)] if early > first else []):
        (sent,) = forecast(ensemble, start, stop - start, fields, halo_early, start, halo_early, early, size, [(0, total)])
        groups.append(sent)
    halo_late = edges(ensemble, early, held - early, (), (groups[0][0],))
    whole = [received(sent) for sent in groups]
    halo_late = tied(halo_late, whole[0])
    sent_late = forecast(ensemble, early, held - early, fields, halo_late, 0, halo_early, early, size, ranges)
    late = [received(sent_late[0]), received(tied(sent_late[1], whole[-1]))]
    late.append(received(tied(sent_late[2], late[0])))

    def woven(pieces, offset):
        return [x for per_source in zip(*whole, pieces) for x in per_source], ([offset] * len(whole) + [0]) * parts

    heights, at = woven(late[0], 0)
    packed = observe(heights, per_field, members, obs_cell, obs_count, obs_value, obs_error)
    packed = lax.psum(packed, ("blk", "sub"))
    mixers = transform(packed, members)
    late += [received(tied(x, late[1], mixers)) for x in sent_late[3:]]
    shape = (members, total, PAD, width)
    out = None
    for (start, stop), pieces in zip(ranges, late):
        out = analyse(mixers, *woven(pieces, start), start, stop, shape, out)
    return out.reshape(members, 3, 1, lines, columns)


def solution(mesh):
    placed = (
        P(("copy", "grid"), None, "blk", "sub"),
        P(("copy", "blk"), "sub"),
        P(("copy", "blk"), "sub"),
        P(("copy", "blk"), "grid", "sub"),
        P(("copy", "blk"), "grid", "sub"),
        P(("copy", "blk"), "grid", "sub"),
        P(("copy", "blk"), "grid", "sub"),
    )
    return jax.shard_map(
        shards,
        mesh=mesh,
        in_specs=placed,
        out_specs=P("copy", None, "blk", "grid", "sub"),
        check_vma=False,
    )
```

```python
import functools
import math

import jax
import jax.numpy as jnp
from jax import lax
from jax.experimental import pallas as pl
from jax.experimental.pallas import tpu as pltpu
from jax.sharding import PartitionSpec as P

STEPS = 2
NS_STEPS = 8
FRICTION = 0.05
PRESSURE = 0.35
DIVERGE = 0.35
CORIOLIS = 0.2
HALO = 2 * STEPS
PAD = 8
LANES = 128
f32 = jnp.float32


def cost(us):
    return pl.CostEstimate(flops=int(us * 1e6), transcendentals=0, bytes_accessed=int(us * 3e3))


def tied(values, *earlier):
    return lax.optimization_barrier((values, earlier))[0]


def thirds(x):
    top = x.astype(jnp.bfloat16)
    x = x - top.astype(f32)
    middle = x.astype(jnp.bfloat16)
    return top, middle, (x - middle.astype(f32)).astype(jnp.bfloat16)


def product(a, b, dims):
    dot = lambda x, y: lax.dot_general(x, y, (dims, ((), ())), preferred_element_type=f32)
    if a.dtype == jnp.bfloat16:
        return dot(a, b)
    (a0, a1, a2), (b0, b1, b2) = thirds(a), thirds(b)
    return ((dot(a2, b0) + dot(a0, b2)) + dot(a1, b1)) + (dot(a1, b0) + dot(a0, b1)) + dot(a0, b0)


def nt(a, b):
    return product(a, b, ((1,), (1,)))


def nn(a, b):
    return product(a, b, ((1,), (0,)))


def pack_kernel(*refs, chunk, two, statics, waits):
    ens_head, ens_tail, ens_first, ens_last, ens_hf, ens_hl, ens_tf, ens_tl = refs[:8]
    outs = refs[8 + (2 if statics else 0) + waits :]
    b, s = lax.axis_index("blk"), lax.axis_index("sub")

    def emit(head, tail, first, last, corner_head, corner_tail, i, index):
        if two:
            outs[0][i, index] = jnp.where(b == 0, tail, head)
            outs[1][i, index] = jnp.where(b == 0, corner_tail, corner_head)
        else:
            outs[0][i, index] = head
            outs[1][i, index] = corner_head
            outs[2][i, index] = tail
            outs[3][i, index] = corner_tail
        outs[-1][i, index] = jnp.where(s == 0, last, first)

    for i in range(chunk):
        for field in range(3):
            emit(
                ens_head[i, field, :HALO],
                ens_tail[i, field, PAD - HALO :],
                ens_first[i, field],
                ens_last[i, field],
                jnp.where(s == 0, ens_hl[i, field, :HALO], ens_hf[i, field, :HALO]),
                jnp.where(s == 0, ens_tl[i, field, PAD - HALO :], ens_tf[i, field, PAD - HALO :]),
                i,
                field,
            )
    if statics:
        for index, source in enumerate((refs[8][...], refs[9][...].astype(f32))):
            rows, columns = source.shape
            head, tail = source[:HALO], source[rows - HALO :]
            first, last = source[:, :LANES], source[:, columns - LANES :]
            emit(
                head,
                tail,
                first,
                last,
                jnp.where(s == 0, head[:, columns - LANES :], head[:, :LANES]),
                jnp.where(s == 0, tail[:, columns - LANES :], tail[:, :LANES]),
                chunk,
                index,
            )


def edges(ensemble, first, members, statics, after):
    rows, columns = ensemble.shape[2:]
    two = lax.axis_size("blk") == 2
    chunk = math.gcd(first, members) if not statics else members
    held = members + (1 if statics else 0)
    block = chunk + (1 if statics else 0)
    row_end, column_end = rows // PAD - 1, columns // LANES - 1

    def taken(shape, r, c):
        return pl.BlockSpec((chunk, 3) + shape, lambda i: (first // chunk + i, 0, r, c))

    in_specs = [
        taken((PAD, columns), 0, 0),
        taken((PAD, columns), row_end, 0),
        taken((rows, LANES), 0, 0),
        taken((rows, LANES), 0, column_end),
        taken((PAD, LANES), 0, 0),
        taken((PAD, LANES), 0, column_end),
        taken((PAD, LANES), row_end, 0),
        taken((PAD, LANES), row_end, column_end),
    ]
    in_specs += [pl.BlockSpec((rows, columns), lambda i: (0, 0))] * len(statics)
    in_specs += [pl.BlockSpec(memory_space=pl.ANY)] * len(after)
    shapes = [(3, HALO, columns), (3, HALO, LANES)] * (1 if two else 2) + [(3, rows, LANES)]
    packed = pl.pallas_call(
        functools.partial(pack_kernel, chunk=chunk, two=two, statics=bool(statics), waits=len(after)),
        grid=(members // chunk,),
        in_specs=in_specs,
        out_specs=[pl.BlockSpec((block,) + s, lambda i: (i, 0, 0, 0)) for s in shapes],
        out_shape=[jax.ShapeDtypeStruct((held,) + s, f32) for s in shapes],
        cost_estimate=cost(3),
        name="edges",
    )(*[ensemble] * 8, *statics, *after)
    return packed


def halo(packed):
    count = lax.axis_size("blk")
    beside = lax.ppermute(packed[-1], "sub", [(0, 1), (1, 0)])
    if count == 2:
        lines = lax.ppermute(packed[0], "blk", [(0, 1), (1, 0)])
        corners = lax.ppermute(packed[1], ("blk", "sub"), [(0, 3), (3, 0), (1, 2), (2, 1)])
        return lines, lines, beside, corners, corners
    up = [(i + 1, i) for i in range(count - 1)]
    down = [(i, i + 1) for i in range(count - 1)]
    below = lax.ppermute(packed[0], "blk", up)
    above = lax.ppermute(packed[2], "blk", down)
    cross = lambda pairs: [(2 * i + s, 2 * j + 1 - s) for i, j in pairs for s in (0, 1)]
    corners_below = lax.ppermute(packed[1], ("blk", "sub"), cross(up))
    corners_above = lax.ppermute(packed[3], ("blk", "sub"), cross(down))
    return below, above, beside, corners_below, corners_above


def forecast_kernel(*refs, parts, tiles, lines, ranges):
    ens, thick, wet = refs[:3]
    mem_halo, sta_halo = refs[3:8], refs[8:13]
    n_out = parts * len(ranges)
    outs = refs[13 : 13 + n_out]
    h, u, v, fu, g, m95, mf, m35, t35, inside, res = refs[13 + n_out :]
    rows, columns = thick.shape
    height, width = h.shape
    z, b, s = lax.axis_index("grid"), lax.axis_index("blk"), lax.axis_index("sub")
    lane = lax.broadcasted_iota(jnp.int32, (1, LANES), 1)
    beside_ok = jnp.where(lax.div(lane, LANES // 2) == s, 1.0, 0.0)
    below_ok = (b < tiles - 1).astype(f32)
    above_ok = (b > 0).astype(f32)
    lower = rows + PAD

    def place(ref, center, below, above, beside, corner_below, corner_above):
        ref[PAD:lower, :columns] = center
        ref[PAD:lower, columns:] = beside * beside_ok
        ref[lower : lower + HALO, :columns] = below * below_ok
        ref[PAD - HALO : PAD, :columns] = above * above_ok
        ref[lower : lower + HALO, columns:] = corner_below * beside_ok * below_ok
        ref[PAD - HALO : PAD, columns:] = corner_above * beside_ok * above_ok

    @pl.when(pl.program_id(0) == 0)
    def _():
        for ref in (h, u, v, m95, t35, inside):
            ref[:PAD] = jnp.zeros((PAD, width), f32)
            ref[lower:] = jnp.zeros((PAD, width), f32)
        place(t35, thick[...], *(ref[0, 0] for ref in sta_halo))
        place(m95, wet[...].astype(f32), *(ref[0, 1] for ref in sta_halo))
        one = lambda *shape: jnp.ones(shape, f32)
        place(inside, one(rows, columns), one(HALO, columns), one(HALO, columns), one(rows, LANES), one(HALO, LANES), one(HALO, LANES))
        for r in range(0, height, PAD):
            here = slice(r, r + PAD)
            t35[here] = DIVERGE * t35[here]
            m = m95[here]
            line = (b * rows + (r - PAD) + lax.broadcasted_iota(jnp.int32, (PAD, 1), 0)).astype(f32)
            m95[here] = (1.0 - FRICTION) * m
            m35[here] = PRESSURE * m
            mf[here] = (CORIOLIS * (2.0 * (line + 0.5) / (tiles * rows) - 1.0)) * m

    for field, ref in enumerate((h, u, v)):
        place(ref, ens[0, field], *(halo_ref[0, field] for halo_ref in mem_halo))

    def above_of(ref, r):
        return pltpu.roll(ref[:PAD], 1, 0) if r == 0 else ref[r - 1 : r - 1 + PAD]

    def below_of(ref, r):
        return pltpu.roll(ref[r : r + PAD], PAD - 1, 0) if r + PAD == height else ref[r + 1 : r + 1 + PAD]

    def across(field):
        return pltpu.roll(field, width - 1, 1) - pltpu.roll(field, 1, 1)

    def keep(field, r, value):
        size = min(PAD, lines)
        for start in range(0, PAD, size):
            domain, line = divmod(r - PAD + start, lines)
            res[field, domain, line : line + size] = value[start : start + size, :columns]

    for step in range(STEPS):
        last = step == STEPS - 1
        for r in range(0, height, PAD):
            here = slice(r, r + PAD)
            hc, uc, vc = h[here], u[here], v[here]
            a, c, d = m95[here], mf[here], m35[here]
            un = a * uc + c * vc - d * (below_of(h, r) - above_of(h, r))
            vn = a * vc - c * uc - d * across(hc)
            t = t35[here]
            fu[here] = t * un
            inner = PAD <= r < lower
            if last and inner:
                keep(1, r, un)
                keep(2, r, vn)
            if not last:
                u[here] = un
                v[here] = vn
            if inner or not last:
                g[here] = across(t * vn)
        for r in range(0, height, PAD):
            here = slice(r, r + PAD)
            if last and not PAD <= r < lower:
                continue
            hn = h[here] - ((below_of(fu, r) - above_of(fu, r)) + g[here])
            if last:
                keep(0, r, hn)
            else:
                h[here] = hn * inside[here]

    per_field = outs[0].shape[1] and lines // outs[0].shape[2]
    for shift in range(parts):
        domain = lax.rem(z + shift, parts)
        for number, (start, stop) in enumerate(ranges):
            out = outs[number * parts + shift]
            for q in range(start, stop):
                field, piece = divmod(q, per_field)
                size = out.shape[2]
                out[0, q - start] = res[field, domain, piece * size : (piece + 1) * size]


def forecast(ensemble, first, members, fields, mem_halo, halo_first, sta_halo, static_at, size, ranges):
    thick, wet = fields
    rows, columns = ensemble.shape[2:]
    parts, tiles = lax.axis_size("grid"), lax.axis_size("blk")
    lines = rows // parts
    ext = pltpu.VMEM((rows + 2 * PAD, columns + LANES), f32)
    whole = pl.BlockSpec((rows, columns), lambda i: (0, 0))
    in_specs = [pl.BlockSpec((1, 3, rows, columns), lambda i: (first + i, 0, 0, 0)), whole, whole]
    in_specs += [pl.BlockSpec((1,) + x.shape[1:], lambda i: (halo_first + i, 0, 0, 0)) for x in mem_halo]
    in_specs += [pl.BlockSpec((1,) + x.shape[1:], lambda i: (static_at, 0, 0, 0)) for x in sta_halo]
    shapes = [(stop - start, size, columns) for start, stop in ranges for shift in range(parts)]
    flat = pl.pallas_call(
        functools.partial(forecast_kernel, parts=parts, tiles=tiles, lines=lines, ranges=ranges),
        grid=(members,),
        in_specs=in_specs,
        out_specs=[pl.BlockSpec((1,) + s, lambda i: (i, 0, 0, 0)) for s in shapes],
        out_shape=[jax.ShapeDtypeStruct((members,) + s, f32) for s in shapes],
        scratch_shapes=[ext] * 10 + [pltpu.VMEM((3, parts, lines, columns), f32)],
        compiler_params=pltpu.CompilerParams(vmem_limit_bytes=48 << 20),
        cost_estimate=cost(3 * members),
        name="forecast",
    )(ensemble, thick, wet, *mem_halo, *sta_halo)
    return [flat[i * parts : (i + 1) * parts] for i in range(len(ranges))]


def exchange(pieces):
    parts = len(pieces)
    got = [pieces[0]]
    for shift in range(1, parts):
        got.append(lax.ppermute(pieces[shift], "grid", [(i, (i + shift) % parts) for i in range(parts)]))
    return got


def rows_of(refs):
    return jnp.concatenate([ref[:, 0].reshape(-1, ref.shape[3]) for ref in refs], axis=0)


def observe_kernel(*refs, members, width):
    count, cell, value, error = refs[:4]
    pieces, (out, picked) = refs[4:-2], refs[-2:]
    q = pl.program_id(0)
    columns = width
    slots = cell.shape[1]
    cells = cell[...]
    column = lax.rem(cells, columns)
    line = lax.rem(lax.div(cells, columns), PAD)
    block = lax.div(cells, columns * PAD)
    chosen = (lax.broadcasted_iota(jnp.int32, (columns, slots), 0) == column) & (block == q)
    pick = jnp.where(chosen, 1.0, 0.0).astype(jnp.bfloat16)
    left = rows_of(pieces)
    found = 0.0
    for part in range(3):
        head = left.astype(jnp.bfloat16)
        found = found + nn(head, pick)
        left = left - head.astype(f32)
    line_of = lax.rem(lax.broadcasted_iota(jnp.int32, found.shape, 0), PAD)
    found = jnp.sum(jnp.where(line_of == line, found, 0.0).reshape(members, PAD, slots), axis=1)

    @pl.when(q == 0)
    def _():
        picked[...] = found

    @pl.when(q > 0)
    def _():
        picked[...] += found

    @pl.when(q == pl.num_programs(0) - 1)
    def _():
        p = picked[...]
        pbar = jnp.mean(p, axis=0, keepdims=True)
        valid = lax.broadcasted_iota(jnp.int32, (1, slots), 1) < count[0, 0]
        scale = jnp.where(valid, 1.0 / (error[...] * math.sqrt(members - 1)), 0.0)
        anomaly = (p - pbar) * scale
        innovation = (value[...] - pbar) * scale
        out[:members] = nt(anomaly, anomaly)
        out[members:] = nt(jnp.broadcast_to(innovation, (PAD, slots)), anomaly)


def piece_specs(pieces, offset):
    return [pl.BlockSpec((x.shape[0], 1) + x.shape[2:], lambda q, o=o: (0, q + o, 0, 0)) for x, o in zip(pieces, offset)]


def observe(pieces, count_q, members, cell, count, value, error):
    slots = cell.shape[-1]
    row = pl.BlockSpec((1, slots), lambda q: (0, 0))
    return pl.pallas_call(
        functools.partial(observe_kernel, members=members, width=pieces[0].shape[3]),
        grid=(count_q,),
        in_specs=[pl.BlockSpec(memory_space=pltpu.SMEM), row, row, row] + piece_specs(pieces, [0] * len(pieces)),
        out_specs=pl.BlockSpec((members + PAD, members), lambda q: (0, 0)),
        out_shape=jax.ShapeDtypeStruct((members + PAD, members), f32),
        scratch_shapes=[pltpu.VMEM((members, slots), f32)],
        cost_estimate=cost(6),
        name="observe",
    )(count.reshape(1, 1), cell.reshape(1, slots), value.reshape(1, slots), error.reshape(1, slots), *pieces)


def transform_kernel(packed, high, low, *, parts, members):
    each = members // parts
    z = lax.axis_index("grid")
    row = lax.broadcasted_iota(jnp.int32, (members, members), 0)
    col = lax.broadcasted_iota(jnp.int32, (members, members), 1)
    eye = jnp.where(row == col, 1.0, 0.0)
    system = eye + packed[:members]
    proj = nt(eye, packed[members:])[:, :1]
    wide = 2 * members
    lane = lax.broadcasted_iota(jnp.int32, (members, wide), 1)
    sub = lax.broadcasted_iota(jnp.int32, (members, wide), 0)
    tableau = jnp.concatenate([system, jnp.broadcast_to(proj, (members, members))], axis=1)

    def eliminate(p, a):
        pivot_row = jnp.sum(jnp.where(sub == p, a, 0.0), axis=0, keepdims=True)
        column = jnp.sum(jnp.where(lane == p, a, 0.0), axis=1, keepdims=True)
        pivot = jnp.sum(jnp.where(lane[:1] == p, pivot_row, 0.0), axis=1, keepdims=True)
        pivot_row = pivot_row / pivot
        return jnp.where(sub == p, pivot_row, a - column * pivot_row)

    tableau = lax.fori_loop(0, members, eliminate, tableau)
    mean_w = jnp.sum(jnp.where(lane == members, tableau, 0.0), axis=1, keepdims=True)
    total = jnp.sum(jnp.sum(system * system, axis=1, keepdims=True), axis=0, keepdims=True)
    scale = jnp.sqrt(total)

    def sweep(_, state):
        y, zz = state
        factor = 1.5 * eye - 0.5 * nn(zz, y)
        return nn(y, factor), nn(factor, zz)

    _, zz = lax.fori_loop(0, NS_STEPS, sweep, (system / scale, eye))
    weights = mean_w + zz / jnp.sqrt(scale)
    mix = weights - jnp.mean(weights, axis=0, keepdims=True) + 1.0 / members
    place, item = lax.div(col, each), lax.rem(col, each)
    true = lax.rem(z - place + parts, parts) * each + item
    mixed = nt(jnp.where(row == true, 1.0, 0.0), mix)
    tall = members * PAD
    spread = jnp.where(
        lax.div(lax.broadcasted_iota(jnp.int32, (tall, members), 0), PAD)
        == lax.broadcasted_iota(jnp.int32, (tall, members), 1),
        1.0,
        0.0,
    ).astype(jnp.bfloat16)
    same = lax.rem(lax.broadcasted_iota(jnp.int32, (tall, tall), 0), PAD) == lax.rem(
        lax.broadcasted_iota(jnp.int32, (tall, tall), 1), PAD
    )
    top = mixed.astype(jnp.bfloat16)
    rest = (mixed - top.astype(f32)).astype(jnp.bfloat16)
    for out, part in ((high, top), (low, rest)):
        tallened = nn(spread, part).astype(jnp.bfloat16)
        out[...] = jnp.where(same, nt(tallened, spread), 0.0).astype(jnp.bfloat16)


def transform(packed, members):
    parts = lax.axis_size("grid")
    tall = members * PAD
    shape = jax.ShapeDtypeStruct((tall, tall), jnp.bfloat16)
    return pl.pallas_call(
        functools.partial(transform_kernel, parts=parts, members=members),
        out_shape=[shape, shape],
        cost_estimate=cost(12),
        name="transform",
    )(packed)


def analysis_kernel(*refs, carried):
    high, low = refs[:2]
    pieces, out = refs[2 : -1 - carried], refs[-1]
    x = rows_of(pieces)
    top = x.astype(jnp.bfloat16)
    rest = (x - top.astype(f32)).astype(jnp.bfloat16)
    y = nn(high[...], rest) + nn(low[...], top)
    y = y + nn(high[...], top)
    out[...] = y.reshape(out.shape)


def analyse(mixers, pieces, offset, q0, q1, shape, carried):
    square = pl.BlockSpec(mixers[0].shape, lambda q: (0, 0))
    specs = [square, square] + piece_specs(pieces, offset)
    operands = [*mixers, *pieces]
    aliases = {}
    if carried is not None:
        aliases = {len(operands): 0}
        specs.append(pl.BlockSpec(memory_space=pl.ANY))
        operands.append(carried)
    return pl.pallas_call(
        functools.partial(analysis_kernel, carried=int(carried is not None)),
        grid=(q1 - q0,),
        in_specs=specs,
        out_specs=pl.BlockSpec((shape[0], 1) + shape[2:], lambda q: (0, q + q0, 0, 0)),
        out_shape=jax.ShapeDtypeStruct(shape, f32),
        input_output_aliases=aliases,
        cost_estimate=cost(2 * (q1 - q0)),
        name="analysis",
    )(*operands)


def shards(ensemble, basin_thickness, wet_indicator, obs_cell, obs_count, obs_value, obs_error):
    held, _, rows, columns = ensemble.shape
    parts = lax.axis_size("grid")
    members = held * parts
    lines = rows // parts
    size = PAD if lines % PAD == 0 else lines
    per_field = lines // size
    total = 3 * per_field
    width = size * columns // PAD
    first, early = max(1, held // 16), max(1, held // 4)
    fields = (basin_thickness, wet_indicator)
    cuts = sorted({0, per_field, 2 * per_field, total - 1, total})
    ranges = list(zip(cuts[:-1], cuts[1:]))

    def received(pieces):
        got = exchange(pieces)
        return [x.reshape(x.shape[0], x.shape[1], PAD, width) for x in got]

    packed_early = edges(ensemble, 0, early, fields, ())
    packed_late = edges(ensemble, early, held - early, (), (packed_early[0],))
    halo_early = halo(packed_early)
    groups = []
    for start, stop in [(0, first)] + ([(first, early)] if early > first else []):
        (sent,) = forecast(ensemble, start, stop - start, fields, halo_early, start, halo_early, early, size, [(0, total)])
        groups.append(sent)
    whole = [received(groups[0])]
    whole += [received(sent) for sent in groups[1:]]
    halo_late = tied(halo(tied(packed_late, halo_early)), whole[0])
    sent_late = forecast(ensemble, early, held - early, fields, halo_late, 0, halo_early, early, size, ranges)
    late = [received(sent_late[0])]
    late.append(received(tied(sent_late[1], whole[-1])))
    late += [received(tied(x, late[0])) for x in sent_late[2:-1]]

    def woven(pieces, offset):
        return [x for per_source in zip(*whole, pieces) for x in per_source], ([offset] * len(whole) + [0]) * parts

    heights, at = woven(late[0], 0)
    packed = observe(heights, per_field, members, obs_cell, obs_count, obs_value, obs_error)
    packed = lax.psum(packed, ("blk", "sub"))
    mixers = transform(packed, members)
    shape = (members, total, PAD, width)
    out = analyse(mixers, *woven(late[0], 0), *ranges[0], shape, None)
    last, out = lax.optimization_barrier((tied(sent_late[-1], late[1]), out))
    late.append(received(last))
    for (start, stop), pieces in list(zip(ranges, late))[1:]:
        out = analyse(mixers, *woven(pieces, start), start, stop, shape, out)
    return out.reshape(members, 3, 1, lines, columns)


def solution(mesh):
    placed = (
        P(("copy", "grid"), None, "blk", "sub"),
        P(("copy", "blk"), "sub"),
        P(("copy", "blk"), "sub"),
        P(("copy", "blk"), "grid", "sub"),
        P(("copy", "blk"), "grid", "sub"),
        P(("copy", "blk"), "grid", "sub"),
        P(("copy", "blk"), "grid", "sub"),
    )
    return jax.shard_map(
        shards,
        mesh=mesh,
        in_specs=placed,
        out_specs=P("copy", None, "blk", "grid", "sub"),
        check_vma=False,
    )
```
